32 devices in a mesh: rows: 4 (over z), cent: 8 (over y, x, core).
Axes of the slice: x: 2, y: 2, z: 4, core: 2. Of those that a mesh axis runs over, the one named last changes fastest.
Arguments:
- train_rows: float32 [16384, 64], P('rows'), may hold values from -6 to 6
- centre_index: int32 [16384], P('cent'), may hold values from 0 to 16383
- precond: bfloat16 [16384, 16384], P('cent', 'rows'), as said below
- coefficients: float32 [16384, 128], P(('rows', 'cent')), may hold values from -6 to 6
- residual: float32 [16384, 128], P(('rows', 'cent')), may hold values from -6 to 6
- direction: float32 [16384, 128], P(('rows', 'cent')), may hold values from -6 to 6
Outputs:
- coef_next: float32 [16384, 128], P(('rows', 'cent'))
- residual_next: float32 [16384, 128], P(('rows', 'cent'))
- direction_next: float32 [16384, 128], P(('rows', 'cent'))
The draws below stay inside these ranges and needn't reach their ends.
Inputs may be any that keep to these rules, and one draw needn't show every extreme that they name: precond is zero below its diagonal.
All inputs are finite; a program needn't handle non-finite values.
Results may differ from the reference program's by a relative error of at most 0.0047.
Values may be sent and summed in bfloat16 or wider, within the bound.
A program may use at most 128 MiB of HBM per device.

```python
import math
import jax
import jax.numpy as jnp
from jax import lax

ROWS_DEV = 4096
CENTRES = 16384
FEAT = 64
OUTS = 128
TRAIN = 16384


def draw_precond(key, part):
    first, second = jax.random.split(jax.random.fold_in(key, 11))
    upper_part = jax.random.normal(first, (CENTRES, CENTRES), jnp.float32) * CENTRES ** (-0.5)
    diag_vals = jnp.exp(jax.random.uniform(second, (CENTRES,), jnp.float32, math.log(0.5), math.log(2.0)))
    row_ids = jnp.arange(CENTRES)[:, None]
    col_ids = jnp.arange(CENTRES)[None, :]
    matrix = jnp.where(col_ids > row_ids, upper_part, 0.0) + jnp.where(col_ids == row_ids, diag_vals[:, None], 0.0)
    return matrix.astype(jnp.bfloat16)


def draw_train_rows(key, part):
    subkeys = jax.random.split(jax.random.fold_in(key, 23), 4)
    groups = max(TRAIN // 64, 2)
    member = jax.random.randint(subkeys[0], (TRAIN,), 0, groups)
    cluster_mean = 1.2 * jax.random.normal(subkeys[1], (groups, FEAT), jnp.float32)
    spread = jnp.full((groups, 1), 0.5, jnp.float32)
    jitter = jax.random.normal(subkeys[3], (TRAIN, FEAT), jnp.float32)
    points = cluster_mean[member] + spread[member] * jitter
    return jnp.clip(points, -6.0, 6.0)


def plant(entries, own_key, least, top_value):
    spot = [jax.random.randint(jax.random.fold_in(own_key, axis), (), 0, length) for axis, length in enumerate(entries.shape)]
    longest = entries.shape.index(max(entries.shape))
    beside = spot[:longest] + [(spot[longest] + 1) % entries.shape[longest]] + spot[longest + 1:]
    return entries.at[tuple(spot)].set(least).at[tuple(beside)].set(top_value)


def levels(own_key, dims, cuts, low, high):
    def one(axis_at, blocks):
        heights = jax.random.uniform(jax.random.fold_in(jax.random.fold_in(own_key, 6), axis_at), (blocks,), jnp.float32, low / len(cuts), high / len(cuts))
        return jnp.repeat(jnp.exp(heights), dims[axis_at] // blocks).reshape((-1,) + (1,) * (len(dims) - axis_at - 1))

    gain = one(*cuts[0])
    for cut in cuts[1:]:
        gain = gain * one(*cut)
    return gain


def scatter_about(own_key, dims, deviation, most, shards=(), held_as=jnp.bfloat16):
    values = deviation * jax.random.normal(own_key, dims, jnp.float32)
    if shards:
        values = values * levels(own_key, dims, shards, -0.22, 0.18)
    return jnp.clip(values, -most, most).astype(held_as)


def setup_inputs(seed: int = 0) -> dict:
    key_of = jax.random.split(jax.random.key(seed), 7)
    return {
        "train_rows": draw_train_rows(jax.random.fold_in(key_of[6], 71), 0),
        "centre_index": plant(jax.random.randint(key_of[1], (CENTRES,), 0, TRAIN), jax.random.fold_in(key_of[1], 1), 0, TRAIN - 1).astype(jnp.int32),
        "precond": draw_precond(jax.random.fold_in(key_of[6], 71), 0),
        "coefficients": scatter_about(key_of[3], (CENTRES, OUTS), 1.0, 6.0, ((0, 32),), jnp.float32),
        "residual": scatter_about(key_of[4], (CENTRES, OUTS), 1.0, 6.0, ((0, 32),), jnp.float32),
        "direction": scatter_about(key_of[5], (CENTRES, OUTS), 1.0, 6.0, ((0, 32),), jnp.float32),
    }


ridge_weight = 0.1


def kernel_tile(block_rows, centres):
    row_sq = jnp.sum(block_rows * block_rows, axis=1)
    cen_sq = jnp.sum(centres * centres, axis=1)
    cross = jnp.dot(block_rows, centres.T, precision=lax.Precision.HIGHEST, preferred_element_type=jnp.float32)
    distance = row_sq[:, None] + cen_sq[None, :] - 2.0 * cross
    return jnp.exp(-(2.0 / FEAT) * distance).astype(jnp.bfloat16)


def reference(train_rows, centre_index, precond, coefficients, residual, direction):
    centres = train_rows[centre_index.astype(jnp.int32)]
    block_size = min(ROWS_DEV, 1024)
    row_blocks = train_rows.reshape(TRAIN // block_size, block_size, FEAT)
    dir_low = direction.astype(jnp.bfloat16)
    coef_field = jnp.dot(precond, dir_low, preferred_element_type=jnp.float32).astype(jnp.bfloat16)

    def forward(block_rows):
        return jnp.dot(kernel_tile(block_rows, centres), coef_field, preferred_element_type=jnp.float32).astype(jnp.bfloat16)

    fitted = lax.map(forward, row_blocks)

    def accumulate(total, pair):
        block_rows, fitted_block = pair
        tile = kernel_tile(block_rows, centres)
        return total + lax.dot_general(tile, fitted_block, (((0,), (0,)), ((), ())), preferred_element_type=jnp.float32), None

    grad, unused = lax.scan(accumulate, jnp.zeros((CENTRES, OUTS), jnp.float32), (row_blocks, fitted))
    grad_low = (grad * (float(TRAIN) ** -0.5)).astype(jnp.bfloat16)
    image = lax.dot_general(precond, grad_low, (((0,), (0,)), ((), ())), preferred_element_type=jnp.float32)
    image = image + ridge_weight * direction
    norm_old = jnp.sum(residual * residual)
    curvature = jnp.sum(direction * image)
    step_size = norm_old / curvature
    coef_next = coefficients + step_size * direction
    residual_next = residual - step_size * image
    norm_new = jnp.sum(residual_next * residual_next)
    direction_next = residual_next + (norm_new / norm_old) * direction
    return coef_next, residual_next, direction_next
```

```python
import functools
import math

import jax
import jax.numpy as jnp
from jax import lax
from jax.experimental import pallas as pl
from jax.experimental.pallas import tpu as pltpu
from jax.sharding import PartitionSpec as P

FEAT = 64
OUTS = 128
CHUNK = 256
F32 = jnp.float32
BF16 = jnp.bfloat16
MESH = pl.DeviceIdType.MESH
POINT_SCALE = math.sqrt(4.0 / FEAT * math.log2(math.e))

ridge_weight = 0.1


def dot(a, b):
    return jnp.dot(a, b, preferred_element_type=F32)


def three(value):
    high = value.astype(BF16)
    rest = value - high.astype(F32)
    middle = rest.astype(BF16)
    low = (rest - middle.astype(F32)).astype(BF16)
    return high.astype(F32), middle.astype(F32), low.astype(F32)


def step_kernel(
    rows_n, cent_n,
    idx_ref, x_ref, p_hbm, res_ref, dir_ref,
    image_ref, sums_ref,
    p_buf, p_sem, k_buf, xaug, xhl_t, caug_t,
    pick, coef, grad, coef_low,
    dir_own, dir_all, fit_own, fit_all, gather_sems,
    fit_acc, fit_rs, img_acc, img_rs,
    sc_own, sc_cent, sc_mid, sc_rows, sc_sems,
):
    z = lax.axis_index("rows")
    me = lax.axis_index("cent")
    core = lax.rem(me, 2)
    chip = lax.div(me, 2)
    other = chip * 2 + (1 - core)
    chips = cent_n // 2
    chunks = p_buf.shape[0]
    rows_here = x_ref.shape[0]
    part = dir_own.shape[0]
    fit_part = fit_acc.shape[1]
    last = rows_n - 1

    def chip_at(distance):
        return lax.rem(chip + distance, chips)

    def p_copy(k):
        return pltpu.make_async_copy(
            p_hbm.at[pl.ds(pl.multiple_of(k * CHUNK, CHUNK), CHUNK)], p_buf.at[k], p_sem.at[k]
        )

    @pl.loop(0, chunks)
    def _(k):
        p_copy(k).start()

    barrier = pltpu.get_barrier_semaphore()
    for d in range(1, cent_n):
        pl.semaphore_signal(
            barrier, inc=1, device_id=(z, lax.rem(me + d, cent_n)), device_id_type=MESH
        )
    for d in range(1, rows_n):
        pl.semaphore_signal(
            barrier, inc=1, device_id=(lax.rem(z + d, rows_n), me), device_id_type=MESH
        )
    dir_own[...] = dir_ref[...].astype(BF16)
    pl.semaphore_wait(barrier, cent_n - 1 + rows_n - 1)

    def gather_copy(which, own, whole, d):
        target = other if d == 0 else chip_at(d) * 2 + core
        return pltpu.make_async_remote_copy(
            src_ref=own, dst_ref=whole.at[me],
            send_sem=gather_sems.at[which, 0, d], recv_sem=gather_sems.at[which, 1, d],
            device_id=(z, target), device_id_type=MESH,
        )

    def forward_copy(which, whole, d):
        source = chip_at(chips - d) * 2 + core
        return pltpu.make_async_remote_copy(
            src_ref=whole.at[source], dst_ref=whole.at[source],
            send_sem=gather_sems.at[which, 2, d], recv_sem=gather_sems.at[which, 3, d],
            device_id=(z, other), device_id_type=MESH,
        )

    def gather_start(which, own, whole):
        for d in list(range(1, chips)) + [0]:
            gather_copy(which, own, whole, d).start()
        whole[me] = own[...]

    def gather_forward(which, own, whole):
        for d in range(1, chips):
            gather_copy(which, own, whole, d).wait_recv()
            forward_copy(which, whole, d).start()

    def gather_end(which, own, whole):
        gather_copy(which, own, whole, 0).wait_recv()
        for d in range(1, chips):
            forward_copy(which, whole, d).wait_recv()
        for d in range(chips):
            gather_copy(which, own, whole, d).wait_send()
        for d in range(1, chips):
            forward_copy(which, whole, d).wait_send()

    def right_copy(scan, k):
        own, to_right, to_left, from_left, from_right, sems = scan
        return pltpu.make_async_remote_copy(
            src_ref=to_right.at[k], dst_ref=from_left.at[k],
            send_sem=sems.at[0, k], recv_sem=sems.at[1, k],
            device_id=(lax.rem(z + 1, rows_n), me), device_id_type=MESH,
        )

    def left_copy(scan, k):
        own, to_right, to_left, from_left, from_right, sems = scan
        return pltpu.make_async_remote_copy(
            src_ref=to_left.at[k], dst_ref=from_right.at[k],
            send_sem=sems.at[2, k], recv_sem=sems.at[3, k],
            device_id=(lax.rem(z + last, rows_n), me), device_id_type=MESH,
        )

    def scan_step(scan, it):
        own, to_right, to_left, from_left, from_right, sems = scan
        kr = it - z
        kl = it - (last - z)

        @pl.when((kr >= 0) & (kr < chunks) & (z < last))
        def _():
            @pl.when(z == 0)
            def _():
                to_right[kr] = own[kr].astype(BF16)

            @pl.when(z > 0)
            def _():
                right_copy(scan, kr).wait_recv()
                to_right[kr] = (own[kr].astype(F32) + from_left[kr].astype(F32)).astype(BF16)

            right_copy(scan, kr).start()

        @pl.when((kl >= 0) & (kl < chunks) & (z > 0))
        def _():
            @pl.when(z == last)
            def _():
                to_left[kl] = own[kl].astype(BF16)

            @pl.when(z < last)
            def _():
                left_copy(scan, kl).wait_recv()
                to_left[kl] = (own[kl].astype(F32) + from_right[kl].astype(F32)).astype(BF16)

            left_copy(scan, kl).start()

    def scan_total(scan, k):
        own, to_right, to_left, from_left, from_right, sems = scan

        @pl.when(z == last)
        def _():
            right_copy(scan, k).wait_recv()

        @pl.when(z == 0)
        def _():
            left_copy(scan, k).wait_recv()

        @pl.when(z > 0)
        def _():
            own[k] = (own[k].astype(F32) + from_left[k].astype(F32)).astype(own.dtype)

        @pl.when(z < last)
        def _():
            own[k] = (own[k].astype(F32) + from_right[k].astype(F32)).astype(own.dtype)

    def scan_sent(scan):
        @pl.loop(0, chunks)
        def _(k):
            @pl.when(z < last)
            def _():
                right_copy(scan, k).wait_send()

            @pl.when(z > 0)
            def _():
                left_copy(scan, k).wait_send()

    def across_copy(buffers, q):
        send_a, recv_a, send_b, recv_b, sems = buffers
        return pltpu.make_async_remote_copy(
            src_ref=send_a.at[q], dst_ref=recv_a.at[q],
            send_sem=sems.at[0, q], recv_sem=sems.at[1, q],
            device_id=(z, other), device_id_type=MESH,
        )

    def between_copy(buffers, d):
        send_a, recv_a, send_b, recv_b, sems = buffers
        return pltpu.make_async_remote_copy(
            src_ref=send_b.at[d], dst_ref=recv_b.at[d],
            send_sem=sems.at[2, d], recv_sem=sems.at[3, d],
            device_id=(z, chip_at(d) * 2 + core), device_id_type=MESH,
        )

    def scatter_sum(acc, buffers):
        send_a, recv_a, send_b, recv_b, sems = buffers
        for d in list(range(1, chips)) + [0]:
            q = chip_at(d)
            send_a[q] = acc[q * 2 + (1 - core)].astype(BF16)
            across_copy(buffers, q).start()
        for d in range(1, chips):
            q = chip_at(d)
            across_copy(buffers, q).wait_recv()
            send_b[d] = (acc[q * 2 + core] + recv_a[q].astype(F32)).astype(BF16)
            between_copy(buffers, d).start()
        across_copy(buffers, chip).wait_recv()
        total = acc[me] + recv_a[chip].astype(F32)
        for d in range(1, chips):
            between_copy(buffers, d).wait_recv()
            total = total + recv_b[d].astype(F32)
        for d in range(chips):
            across_copy(buffers, chip_at(d)).wait_send()
        for d in range(1, chips):
            between_copy(buffers, d).wait_send()
        return total

    gather_start(0, dir_own, dir_all)

    point_block = math.gcd(rows_here, 512)

    @pl.loop(0, rows_here // point_block)
    def _(b):
        here = pl.ds(pl.multiple_of(b * point_block, point_block), point_block)
        points = x_ref[here, :] * POINT_SCALE
        high = points.astype(BF16)
        low = (points - high.astype(F32)).astype(BF16)
        exact = high.astype(F32) + low.astype(F32)
        half = -0.5 * jnp.sum(exact * exact, axis=1, keepdims=True)
        first, second, third = three(half)
        lane = lax.broadcasted_iota(jnp.int32, (point_block, FEAT), 1)
        extra = jnp.where(
            lane == 0, first,
            jnp.where(lane == 1, second, jnp.where(lane == 2, third, jnp.where(lane < 6, 1.0, 0.0))),
        )
        high32 = high.astype(F32)
        low32 = low.astype(F32)
        xaug[here, :] = jnp.concatenate([high32, low32, high32, extra], axis=1).astype(BF16)
        xhl_t[:, here] = jnp.concatenate([high32, low32], axis=1).T.astype(BF16)

    pick_block = math.gcd(rows_here, 1024)

    @pl.loop(0, chunks + rows_n - 1)
    def _(it):
        @pl.when(it < chunks)
        def _():
            wanted = idx_ref[it] - z * rows_here
            total = jnp.zeros((2 * FEAT, CHUNK), F32)
            for b in range(rows_here // pick_block):
                ids = lax.broadcasted_iota(jnp.int32, (pick_block, CHUNK), 0) + b * pick_block
                hot = jnp.where(ids == wanted, 1.0, 0.0).astype(BF16)
                total = total + dot(xhl_t[:, b * pick_block : (b + 1) * pick_block], hot)
            pick[0][it] = total.astype(BF16)

        scan_step(pick, it)

    gather_forward(0, dir_own, dir_all)
    gather_end(0, dir_own, dir_all)

    fit_acc[...] = jnp.zeros_like(fit_acc)
    k_block = math.gcd(rows_here, 512)

    @pl.loop(0, chunks + rows_n - 1)
    def _(it):
        @pl.when(it < chunks)
        def _():
            p_copy(it).wait()
            directions = dir_all[...].reshape(cent_n * part, OUTS)
            coef[0][it] = dot(p_buf[it], directions)

        scan_step(coef, it)

        @pl.when(it < chunks)
        def _():
            scan_total(pick, it)
            pair = pick[0][it].astype(F32)
            high = pair[:FEAT]
            low = pair[FEAT:]
            exact = high + low
            half = -0.5 * jnp.sum(exact * exact, axis=0, keepdims=True)
            first, second, third = three(half)
            sub = lax.broadcasted_iota(jnp.int32, (FEAT, CHUNK), 0)
            extra = jnp.where(
                sub < 3, 1.0,
                jnp.where(sub == 3, first, jnp.where(sub == 4, second, jnp.where(sub == 5, third, 0.0))),
            )
            caug_t[...] = jnp.concatenate([high, high, low, extra], axis=0).astype(BF16)

            @pl.loop(0, rows_here // k_block)
            def _(b):
                here = pl.ds(pl.multiple_of(b * k_block, k_block), k_block)
                k_buf[it, here, :] = jnp.exp2(dot(xaug[here, :], caug_t[...])).astype(BF16)

        @pl.when(it >= rows_n - 1)
        def _():
            k = it - (rows_n - 1)
            scan_total(coef, k)
            coef_low[...] = coef[0][k].astype(BF16)

            @pl.loop(0, cent_n)
            def _(b):
                here = pl.ds(pl.multiple_of(b * fit_part, fit_part), fit_part)
                fit_acc[b] += dot(k_buf[k, here, :], coef_low[...])

    fitted = scatter_sum(fit_acc, fit_rs)
    fit_own[...] = fitted.T.astype(BF16)
    gather_start(1, fit_own, fit_all)
    img_acc[...] = jnp.zeros_like(img_acc)
    gather_forward(1, fit_own, fit_all)
    gather_end(1, fit_own, fit_all)

    scale = float(rows_here * rows_n) ** -0.5

    @pl.loop(0, chunks + rows_n - 1)
    def _(it):
        @pl.when(it < chunks)
        def _():
            total = jnp.zeros((OUTS, CHUNK), F32)
            for b in range(cent_n):
                total = total + dot(
                    fit_all[b], k_buf[it, b * fit_part : (b + 1) * fit_part, :]
                )
            grad[0][it] = total

        scan_step(grad, it)

        @pl.when(it >= rows_n - 1)
        def _():
            k = it - (rows_n - 1)
            scan_total(grad, k)
            low = (grad[0][k] * scale).astype(BF16)
            for b in range(cent_n):
                img_acc[b] += dot(low, p_buf[k, :, b * part : (b + 1) * part])

    image = scatter_sum(img_acc, img_rs).T + ridge_weight * dir_ref[...]
    image_ref[...] = image

    def rows_sum(value):
        return jnp.sum(value, axis=0, keepdims=True)

    residual = res_ref[...]
    sc_own[...] = jnp.concatenate(
        [
            rows_sum(residual * residual),
            rows_sum(dir_ref[...] * image),
            rows_sum(residual * image),
            rows_sum(image * image),
            jnp.zeros((4, OUTS), F32),
        ],
        axis=0,
    )

    def cent_copy(d):
        return pltpu.make_async_remote_copy(
            src_ref=sc_own, dst_ref=sc_cent.at[d],
            send_sem=sc_sems.at[0, d], recv_sem=sc_sems.at[1, d],
            device_id=(z, lax.rem(me + d, cent_n)), device_id_type=MESH,
        )

    def rows_copy(d):
        return pltpu.make_async_remote_copy(
            src_ref=sc_mid, dst_ref=sc_rows.at[d],
            send_sem=sc_sems.at[2, d], recv_sem=sc_sems.at[3, d],
            device_id=(lax.rem(z + d, rows_n), me), device_id_type=MESH,
        )

    for d in range(1, cent_n):
        cent_copy(d).start()
    total = sc_own[...]
    for d in range(1, cent_n):
        cent_copy(d).wait_recv()
        total = total + sc_cent[d]
    sc_mid[...] = total
    for d in range(1, rows_n):
        rows_copy(d).start()
    for d in range(1, rows_n):
        rows_copy(d).wait_recv()
        total = total + sc_rows[d]
    sums_ref[...] = total

    for d in range(1, cent_n):
        cent_copy(d).wait_send()
    for d in range(1, rows_n):
        rows_copy(d).wait_send()
    scan_sent(pick)
    scan_sent(coef)
    scan_sent(grad)


def on_device(rows_n, cent_n, train_rows, centre_index, precond, coefficients, residual, direction):
    rows_here = train_rows.shape[0]
    centres_here = centre_index.shape[0]
    part = direction.shape[0]
    chunks = centres_here // CHUNK
    chips = cent_n // 2
    fit_part = rows_here // cent_n
    vmem = pl.BlockSpec(memory_space=pltpu.VMEM)

    def scan(shape, own_dtype):
        piece = (chunks,) + shape
        return (
            pltpu.VMEM(piece, own_dtype),
            pltpu.VMEM(piece, BF16), pltpu.VMEM(piece, BF16),
            pltpu.VMEM(piece, BF16), pltpu.VMEM(piece, BF16),
            pltpu.SemaphoreType.DMA((4, chunks)),
        )

    def scatter(shape):
        piece = (chips,) + shape
        return (
            pltpu.VMEM(piece, BF16), pltpu.VMEM(piece, BF16),
            pltpu.VMEM(piece, BF16), pltpu.VMEM(piece, BF16),
            pltpu.SemaphoreType.DMA((4, chips)),
        )

    image, sums = pl.pallas_call(
        functools.partial(step_kernel, rows_n, cent_n),
        out_shape=(
            jax.ShapeDtypeStruct((part, OUTS), F32),
            jax.ShapeDtypeStruct((8, OUTS), F32),
        ),
        in_specs=[vmem, vmem, pl.BlockSpec(memory_space=pl.ANY), vmem, vmem],
        out_specs=(vmem, vmem),
        scratch_shapes=[
            pltpu.VMEM((chunks, CHUNK, precond.shape[1]), BF16),
            pltpu.SemaphoreType.DMA((chunks,)),
            pltpu.VMEM((chunks, rows_here, CHUNK), BF16),
            pltpu.VMEM((rows_here, 4 * FEAT), BF16),
            pltpu.VMEM((2 * FEAT, rows_here), BF16),
            pltpu.VMEM((4 * FEAT, CHUNK), BF16),
            scan((2 * FEAT, CHUNK), BF16),
            scan((CHUNK, OUTS), F32),
            scan((OUTS, CHUNK), F32),
            pltpu.VMEM((CHUNK, OUTS), BF16),
            pltpu.VMEM((part, OUTS), BF16),
            pltpu.VMEM((cent_n, part, OUTS), BF16),
            pltpu.VMEM((OUTS, fit_part), BF16),
            pltpu.VMEM((cent_n, OUTS, fit_part), BF16),
            pltpu.SemaphoreType.DMA((2, 4, chips)),
            pltpu.VMEM((cent_n, fit_part, OUTS), F32),
            scatter((fit_part, OUTS)),
            pltpu.VMEM((cent_n, OUTS, part), F32),
            scatter((OUTS, part)),
            pltpu.VMEM((8, OUTS), F32),
            pltpu.VMEM((cent_n, 8, OUTS), F32),
            pltpu.VMEM((8, OUTS), F32),
            pltpu.VMEM((rows_n, 8, OUTS), F32),
            pltpu.SemaphoreType.DMA((4, max(cent_n, rows_n))),
        ],
        compiler_params=pltpu.CompilerParams(
            collective_id=0, has_side_effects=True, vmem_limit_bytes=67000000
        ),
        name="falkon_step",
    )(centre_index.reshape(chunks, 1, CHUNK), train_rows, precond, residual, direction)

    totals = jnp.sum(sums, axis=1)
    norm_old, curvature, cross, square = totals[0], totals[1], totals[2], totals[3]
    step_size = norm_old / curvature
    norm_new = norm_old - 2.0 * step_size * cross + step_size * step_size * square
    coef_next = coefficients + step_size * direction
    residual_next = residual - step_size * image
    direction_next = residual_next + norm_new / norm_old * direction
    return (coef_next, residual_next, direction_next)


def solution(mesh):
    both = P(("rows", "cent"), None)
    return jax.shard_map(
        functools.partial(on_device, mesh.shape["rows"], mesh.shape["cent"]),
        mesh=mesh,
        in_specs=(P("rows", None), P("cent"), P("cent", "rows"), both, both, both),
        out_specs=(both, both, both),
        check_vma=False,
    )
```

```python
import functools
import math

import jax
import jax.numpy as jnp
from jax import lax
from jax.experimental import pallas as pl
from jax.experimental.pallas import tpu as pltpu
from jax.sharding import PartitionSpec as P

FEAT = 64
OUTS = 128
CHUNK = 256
LAG = 2
F32 = jnp.float32
BF16 = jnp.bfloat16
MESH = pl.DeviceIdType.MESH
POINT_SCALE = math.sqrt(4.0 / FEAT)

ridge_weight = 0.1


def dot(a, b):
    return jnp.dot(a, b, preferred_element_type=F32)


def three(value):
    high = value.astype(BF16)
    rest = value - high.astype(F32)
    middle = rest.astype(BF16)
    low = (rest - middle.astype(F32)).astype(BF16)
    return high.astype(F32), middle.astype(F32), low.astype(F32)


def step_kernel(
    rows_n, cent_n,
    idx_ref, x_ref, p_hbm, res_ref, dir_ref,
    image_ref, sums_ref,
    p_buf, p_sem, k_buf, xaug, xhl_t, caug_t,
    pick, coef, grad, coef_low,
    dir_own, dir_all, fit_own, fit_all, gather_sems,
    fit_acc, fit_rs, img_acc, img_rs,
    sc_own, sc_cent, sc_mid, sc_rows, sc_sems,
):
    z = lax.axis_index("rows")
    me = lax.axis_index("cent")
    core = lax.rem(me, 2)
    chip = lax.div(me, 2)
    other = chip * 2 + (1 - core)
    chips = cent_n // 2
    chunks = p_buf.shape[0]
    rows_here = x_ref.shape[1]
    part = dir_own.shape[0]
    fit_part = fit_acc.shape[1]
    last = rows_n - 1

    def chip_at(distance):
        return lax.rem(chip + distance, chips)

    def p_copy(k):
        return pltpu.make_async_copy(
            p_hbm.at[pl.ds(pl.multiple_of(k * CHUNK, CHUNK), CHUNK)], p_buf.at[k], p_sem.at[k]
        )

    @pl.loop(0, chunks)
    def _(k):
        p_copy(k).start()

    barrier = pltpu.get_barrier_semaphore()
    for d in range(1, cent_n):
        pl.semaphore_signal(
            barrier, inc=1, device_id=(z, lax.rem(me + d, cent_n)), device_id_type=MESH
        )
    for d in range(1, rows_n):
        pl.semaphore_signal(
            barrier, inc=1, device_id=(lax.rem(z + d, rows_n), me), device_id_type=MESH
        )
    dir_own[...] = dir_ref[...].astype(BF16)
    pl.semaphore_wait(barrier, cent_n - 1 + rows_n - 1)

    def gather_copy(which, own, whole, d):
        target = other if d == 0 else chip_at(d) * 2 + core
        return pltpu.make_async_remote_copy(
            src_ref=own, dst_ref=whole.at[me],
            send_sem=gather_sems.at[which, 0, d], recv_sem=gather_sems.at[which, 1, d],
            device_id=(z, target), device_id_type=MESH,
        )

    def forward_copy(which, whole, d):
        source = chip_at(chips - d) * 2 + core
        return pltpu.make_async_remote_copy(
            src_ref=whole.at[source], dst_ref=whole.at[source],
            send_sem=gather_sems.at[which, 2, d], recv_sem=gather_sems.at[which, 3, d],
            device_id=(z, other), device_id_type=MESH,
        )

    def gather_start(which, own, whole):
        for d in list(range(1, chips)) + [0]:
            gather_copy(which, own, whole, d).start()
        whole[me] = own[...]

    def gather_forward(which, own, whole):
        for d in range(1, chips):
            gather_copy(which, own, whole, d).wait_recv()
            forward_copy(which, whole, d).start()

    def gather_end(which, own, whole):
        gather_copy(which, own, whole, 0).wait_recv()
        for d in range(1, chips):
            forward_copy(which, whole, d).wait_recv()
        for d in range(chips):
            gather_copy(which, own, whole, d).wait_send()
        for d in range(1, chips):
            forward_copy(which, whole, d).wait_send()

    def right_copy(scan, k):
        own, to_right, to_left, from_left, from_right, sems = scan
        return pltpu.make_async_remote_copy(
            src_ref=to_right.at[k], dst_ref=from_left.at[k],
            send_sem=sems.at[0, k], recv_sem=sems.at[1, k],
            device_id=(lax.rem(z + 1, rows_n), me), device_id_type=MESH,
        )

    def left_copy(scan, k):
        own, to_right, to_left, from_left, from_right, sems = scan
        return pltpu.make_async_remote_copy(
            src_ref=to_left.at[k], dst_ref=from_right.at[k],
            send_sem=sems.at[2, k], recv_sem=sems.at[3, k],
            device_id=(lax.rem(z + last, rows_n), me), device_id_type=MESH,
        )

    def scan_step(scan, it):
        own, to_right, to_left, from_left, from_right, sems = scan
        kr = it - LAG * z
        kl = it - LAG * (last - z)

        @pl.when((kr >= 0) & (kr < chunks) & (z < last))
        def _():
            @pl.when(z == 0)
            def _():
                to_right[kr] = own[kr].astype(BF16)

            @pl.when(z > 0)
            def _():
                right_copy(scan, kr).wait_recv()
                to_right[kr] = (own[kr].astype(F32) + from_left[kr].astype(F32)).astype(BF16)

            right_copy(scan, kr).start()

        @pl.when((kl >= 0) & (kl < chunks) & (z > 0))
        def _():
            @pl.when(z == last)
            def _():
                to_left[kl] = own[kl].astype(BF16)

            @pl.when(z < last)
            def _():
                left_copy(scan, kl).wait_recv()
                to_left[kl] = (own[kl].astype(F32) + from_right[kl].astype(F32)).astype(BF16)

            left_copy(scan, kl).start()

    def scan_total(scan, k):
        own, to_right, to_left, from_left, from_right, sems = scan

        @pl.when(z == last)
        def _():
            right_copy(scan, k).wait_recv()

        @pl.when(z == 0)
        def _():
            left_copy(scan, k).wait_recv()

        @pl.when(z > 0)
        def _():
            own[k] = (own[k].astype(F32) + from_left[k].astype(F32)).astype(own.dtype)

        @pl.when(z < last)
        def _():
            own[k] = (own[k].astype(F32) + from_right[k].astype(F32)).astype(own.dtype)

    def scan_sent(scan):
        @pl.loop(0, chunks)
        def _(k):
            @pl.when(z < last)
            def _():
                right_copy(scan, k).wait_send()

            @pl.when(z > 0)
            def _():
                left_copy(scan, k).wait_send()

    def across_copy(buffers, q):
        send_a, recv_a, send_b, recv_b, sems = buffers
        return pltpu.make_async_remote_copy(
            src_ref=send_a.at[q], dst_ref=recv_a.at[q],
            send_sem=sems.at[0, q], recv_sem=sems.at[1, q],
            device_id=(z, other), device_id_type=MESH,
        )

    def between_copy(buffers, d):
        send_a, recv_a, send_b, recv_b, sems = buffers
        return pltpu.make_async_remote_copy(
            src_ref=send_b.at[d], dst_ref=recv_b.at[d],
            send_sem=sems.at[2, d], recv_sem=sems.at[3, d],
            device_id=(z, chip_at(d) * 2 + core), device_id_type=MESH,
        )

    def scatter_sum(acc, buffers):
        send_a, recv_a, send_b, recv_b, sems = buffers
        for d in list(range(1, chips)) + [0]:
            q = chip_at(d)
            send_a[q] = acc[q * 2 + (1 - core)].astype(BF16)
            across_copy(buffers, q).start()
        for d in range(1, chips):
            q = chip_at(d)
            across_copy(buffers, q).wait_recv()
            send_b[d] = (acc[q * 2 + core] + recv_a[q].astype(F32)).astype(BF16)
            between_copy(buffers, d).start()
        across_copy(buffers, chip).wait_recv()
        total = acc[me] + recv_a[chip].astype(F32)
        for d in range(1, chips):
            between_copy(buffers, d).wait_recv()
            total = total + recv_b[d].astype(F32)
        for d in range(chips):
            across_copy(buffers, chip_at(d)).wait_send()
        for d in range(1, chips):
            between_copy(buffers, d).wait_send()
        return total

    gather_start(0, dir_own, dir_all)

    point_block = rows_here // chunks

    for b in range(chunks):
        here = slice(b * point_block, (b + 1) * point_block)
        points = x_ref[:, here] * POINT_SCALE
        high = points.astype(BF16)
        xhl_t[:FEAT, here] = high
        xhl_t[FEAT:, here] = (points - high.astype(F32)).astype(BF16)

    def augmented(pair, norm_at, one_at):
        high = pair[:FEAT]
        low = pair[FEAT:]
        exact = high + low
        half = -0.5 * jnp.sum(exact * exact, axis=0, keepdims=True)
        sub = lax.broadcasted_iota(jnp.int32, high.shape, 0)
        extra = jnp.where((sub >= one_at) & (sub < one_at + 3), 1.0, 0.0)
        for at, term in enumerate(three(half)):
            extra = jnp.where(sub == norm_at + at, term, extra)
        return high, low, extra

    def augment(b):
        here = pl.ds(pl.multiple_of(b * point_block, point_block), point_block)
        high, low, extra = augmented(xhl_t[:, here].astype(F32), 0, 3)
        xaug[here, :] = jnp.concatenate([high, low, high, extra], axis=0).T.astype(BF16)

    pick_block = math.gcd(rows_here, 1024)

    @pl.loop(0, chunks)
    def _(it):
        wanted = idx_ref[it] - z * rows_here
        total = jnp.zeros((2 * FEAT, CHUNK), F32)
        for b in range(rows_here // pick_block):
            ids = lax.broadcasted_iota(jnp.int32, (pick_block, CHUNK), 0) + b * pick_block
            hot = jnp.where(ids == wanted, 1.0, 0.0).astype(BF16)
            total = total + dot(xhl_t[:, b * pick_block : (b + 1) * pick_block], hot)
        pick[0][it] = total.astype(BF16)
        scan_step(pick, it)
        augment(it)

    gather_forward(0, dir_own, dir_all)
    gather_end(0, dir_own, dir_all)

    fit_acc[...] = jnp.zeros_like(fit_acc)
    k_block = math.gcd(rows_here, 512)

    @pl.loop(0, chunks + LAG * last)
    def _(it):
        scan_step(pick, it + chunks)

        @pl.when(it < chunks)
        def _():
            p_copy(it).wait()
            directions = dir_all[...].reshape(cent_n * part, OUTS)
            coef[0][it] = dot(p_buf[it], directions)

        scan_step(coef, it)

        @pl.when(it < chunks)
        def _():
            scan_total(pick, it)
            high, low, extra = augmented(pick[0][it].astype(F32), 3, 0)
            caug_t[...] = jnp.concatenate([high, high, low, extra], axis=0).astype(BF16)

            for b in range(rows_here // k_block):
                here = slice(b * k_block, (b + 1) * k_block)
                k_buf[it, here, :] = jnp.exp(dot(xaug[here, :], caug_t[...])).astype(BF16)

        @pl.when(it >= LAG * last)
        def _():
            k = it - LAG * last
            scan_total(coef, k)
            coef_low[...] = coef[0][k].astype(BF16)

            for b in range(cent_n):
                here = slice(b * fit_part, (b + 1) * fit_part)
                fit_acc[b] += dot(k_buf[k, here, :], coef_low[...])

    fitted = scatter_sum(fit_acc, fit_rs)
    fit_own[...] = fitted.T.astype(BF16)
    gather_start(1, fit_own, fit_all)
    img_acc[...] = jnp.zeros_like(img_acc)
    gather_forward(1, fit_own, fit_all)
    gather_end(1, fit_own, fit_all)

    scale = float(rows_here * rows_n) ** -0.5

    @pl.loop(0, chunks + LAG * last)
    def _(it):
        @pl.when(it < chunks)
        def _():
            total = jnp.zeros((OUTS, CHUNK), F32)
            for b in range(cent_n):
                total = total + dot(
                    fit_all[b], k_buf[it, b * fit_part : (b + 1) * fit_part, :]
                )
            grad[0][it] = total

        scan_step(grad, it)

        @pl.when(it >= LAG * last)
        def _():
            k = it - LAG * last
            scan_total(grad, k)
            low = (grad[0][k] * scale).astype(BF16)
            for b in range(cent_n):
                img_acc[b] += dot(low, p_buf[k, :, b * part : (b + 1) * part])

    image = scatter_sum(img_acc, img_rs).T + ridge_weight * dir_ref[...]
    image_ref[...] = image

    def rows_sum(value):
        return jnp.sum(value, axis=0, keepdims=True)

    residual = res_ref[...]
    sc_own[...] = jnp.concatenate(
        [
            rows_sum(residual * residual),
            rows_sum(dir_ref[...] * image),
            rows_sum(residual * image),
            rows_sum(image * image),
            jnp.zeros((4, OUTS), F32),
        ],
        axis=0,
    )

    def cent_copy(d):
        return pltpu.make_async_remote_copy(
            src_ref=sc_own, dst_ref=sc_cent.at[d],
            send_sem=sc_sems.at[0, d], recv_sem=sc_sems.at[1, d],
            device_id=(z, lax.rem(me + d, cent_n)), device_id_type=MESH,
        )

    def rows_copy(d):
        return pltpu.make_async_remote_copy(
            src_ref=sc_mid, dst_ref=sc_rows.at[d],
            send_sem=sc_sems.at[2, d], recv_sem=sc_sems.at[3, d],
            device_id=(lax.rem(z + d, rows_n), me), device_id_type=MESH,
        )

    for d in range(1, cent_n):
        cent_copy(d).start()
    total = sc_own[...]
    for d in range(1, cent_n):
        cent_copy(d).wait_recv()
        total = total + sc_cent[d]
    sc_mid[...] = total
    for d in range(1, rows_n):
        rows_copy(d).start()
    for d in range(1, rows_n):
        rows_copy(d).wait_recv()
        total = total + sc_rows[d]
    sums_ref[...] = total

    for d in range(1, cent_n):
        cent_copy(d).wait_send()
    for d in range(1, rows_n):
        rows_copy(d).wait_send()
    scan_sent(pick)
    scan_sent(coef)
    scan_sent(grad)


def update_kernel(sums_ref, image_ref, coef_ref, res_ref, dir_ref, coef_out, res_out, dir_out):
    totals = jnp.sum(sums_ref[...], axis=1, keepdims=True)
    norm_old, curvature, cross, square = (totals[at : at + 1] for at in range(4))
    step_size = norm_old / curvature
    norm_new = norm_old - 2.0 * step_size * cross + step_size * step_size * square
    ratio = norm_new / norm_old
    direction = dir_ref[...]
    coef_out[...] = coef_ref[...] + step_size * direction
    residual_next = res_ref[...] - step_size * image_ref[...]
    res_out[...] = residual_next
    dir_out[...] = residual_next + ratio * direction


def on_device(rows_n, cent_n, train_rows, centre_index, precond, coefficients, residual, direction):
    rows_here = train_rows.shape[0]
    centres_here = centre_index.shape[0]
    part = direction.shape[0]
    chunks = centres_here // CHUNK
    chips = cent_n // 2
    fit_part = rows_here // cent_n
    vmem = pl.BlockSpec(memory_space=pltpu.VMEM)

    def scan(shape, own_dtype):
        piece = (chunks,) + shape
        return (
            pltpu.VMEM(piece, own_dtype),
            pltpu.VMEM(piece, BF16), pltpu.VMEM(piece, BF16),
            pltpu.VMEM(piece, BF16), pltpu.VMEM(piece, BF16),
            pltpu.SemaphoreType.DMA((4, chunks)),
        )

    def scatter(shape):
        piece = (chips,) + shape
        return (
            pltpu.VMEM(piece, BF16), pltpu.VMEM(piece, BF16),
            pltpu.VMEM(piece, BF16), pltpu.VMEM(piece, BF16),
            pltpu.SemaphoreType.DMA((4, chips)),
        )

    image, sums = pl.pallas_call(
        functools.partial(step_kernel, rows_n, cent_n),
        out_shape=(
            jax.ShapeDtypeStruct((part, OUTS), F32),
            jax.ShapeDtypeStruct((8, OUTS), F32),
        ),
        in_specs=[vmem, vmem, pl.BlockSpec(memory_space=pl.ANY), vmem, vmem],
        out_specs=(vmem, vmem),
        scratch_shapes=[
            pltpu.VMEM((chunks, CHUNK, precond.shape[1]), BF16),
            pltpu.SemaphoreType.DMA((chunks,)),
            pltpu.VMEM((chunks, rows_here, CHUNK), BF16),
            pltpu.VMEM((rows_here, 4 * FEAT), BF16),
            pltpu.VMEM((2 * FEAT, rows_here), BF16),
            pltpu.VMEM((4 * FEAT, CHUNK), BF16),
            scan((2 * FEAT, CHUNK), BF16),
            scan((CHUNK, OUTS), F32),
            scan((OUTS, CHUNK), F32),
            pltpu.VMEM((CHUNK, OUTS), BF16),
            pltpu.VMEM((part, OUTS), BF16),
            pltpu.VMEM((cent_n, part, OUTS), BF16),
            pltpu.VMEM((OUTS, fit_part), BF16),
            pltpu.VMEM((cent_n, OUTS, fit_part), BF16),
            pltpu.SemaphoreType.DMA((2, 4, chips)),
            pltpu.VMEM((cent_n, fit_part, OUTS), F32),
            scatter((fit_part, OUTS)),
            pltpu.VMEM((cent_n, OUTS, part), F32),
            scatter((OUTS, part)),
            pltpu.VMEM((8, OUTS), F32),
            pltpu.VMEM((cent_n, 8, OUTS), F32),
            pltpu.VMEM((8, OUTS), F32),
            pltpu.VMEM((rows_n, 8, OUTS), F32),
            pltpu.SemaphoreType.DMA((4, max(cent_n, rows_n))),
        ],
        compiler_params=pltpu.CompilerParams(
            collective_id=0, has_side_effects=True, vmem_limit_bytes=67000000
        ),
        name="falkon_step",
    )(centre_index.reshape(chunks, 1, CHUNK), train_rows.T, precond, residual, direction)

    piece = jax.ShapeDtypeStruct((part, OUTS), F32)
    return pl.pallas_call(
        update_kernel,
        out_shape=(piece, piece, piece),
        in_specs=[vmem] * 5,
        out_specs=(vmem, vmem, vmem),
        name="falkon_update",
    )(sums, image, coefficients, residual, direction)


def solution(mesh):
    both = P(("rows", "cent"), None)
    return jax.shard_map(
        functools.partial(on_device, mesh.shape["rows"], mesh.shape["cent"]),
        mesh=mesh,
        in_specs=(P("rows", None), P("cent"), P("cent", "rows"), both, both, both),
        out_specs=(both, both, both),
        check_vma=False,
    )
```

```python
import functools
import math

import jax
import jax.numpy as jnp
from jax import lax
from jax.experimental import pallas as pl
from jax.experimental.pallas import tpu as pltpu
from jax.sharding import PartitionSpec as P

FEAT = 64
OUTS = 128
CHUNK = 256
LAG = 3
F32 = jnp.float32
BF16 = jnp.bfloat16
MESH = pl.DeviceIdType.MESH
POINT_SCALE = math.sqrt(4.0 / FEAT)

ridge_weight = 0.1


def dot(a, b):
    return jnp.dot(a, b, preferred_element_type=F32)


def three(value):
    high = value.astype(BF16)
    rest = value - high.astype(F32)
    middle = rest.astype(BF16)
    low = (rest - middle.astype(F32)).astype(BF16)
    return high.astype(F32), middle.astype(F32), low.astype(F32)


def step_kernel(
    rows_n, cent_n,
    idx_ref, x_ref, p_hbm, res_ref, dir_ref,
    image_ref, sums_ref,
    p_buf, p_sem, k_buf, xaug, xhl_t, caug_t,
    pick, coef, grad, coef_low,
    dir_own, dir_all, fit_own, fit_all, gather_sems,
    fit_acc, fit_rs, img_acc, img_rs,
    sc_own, sc_cent, sc_mid, sc_rows, sc_sems,
):
    z = lax.axis_index("rows")
    me = lax.axis_index("cent")
    core = lax.rem(me, 2)
    chip = lax.div(me, 2)
    other = chip * 2 + (1 - core)
    chips = cent_n // 2
    chunks = p_buf.shape[0]
    rows_here = x_ref.shape[1]
    part = dir_own.shape[0]
    fit_part = fit_acc.shape[1]
    last = rows_n - 1

    def chip_at(distance):
        return lax.rem(chip + distance, chips)

    def p_copy(k):
        return pltpu.make_async_copy(
            p_hbm.at[pl.ds(pl.multiple_of(k * CHUNK, CHUNK), CHUNK)], p_buf.at[k], p_sem.at[k]
        )

    @pl.loop(0, chunks)
    def _(k):
        p_copy(k).start()

    barrier = pltpu.get_barrier_semaphore()
    for d in range(1, cent_n):
        pl.semaphore_signal(
            barrier, inc=1, device_id=(z, lax.rem(me + d, cent_n)), device_id_type=MESH
        )
    for d in range(1, rows_n):
        pl.semaphore_signal(
            barrier, inc=1, device_id=(lax.rem(z + d, rows_n), me), device_id_type=MESH
        )
    dir_own[...] = dir_ref[...].astype(BF16)
    pl.semaphore_wait(barrier, cent_n - 1 + rows_n - 1)

    def gather_copy(which, own, whole, d):
        target = other if d == 0 else chip_at(d) * 2 + core
        return pltpu.make_async_remote_copy(
            src_ref=own, dst_ref=whole.at[me],
            send_sem=gather_sems.at[which, 0, d], recv_sem=gather_sems.at[which, 1, d],
            device_id=(z, target), device_id_type=MESH,
        )

    def forward_copy(which, whole, d):
        source = chip_at(chips - d) * 2 + core
        return pltpu.make_async_remote_copy(
            src_ref=whole.at[source], dst_ref=whole.at[source],
            send_sem=gather_sems.at[which, 2, d], recv_sem=gather_sems.at[which, 3, d],
            device_id=(z, other), device_id_type=MESH,
        )

    def gather_start(which, own, whole):
        for d in list(range(1, chips)) + [0]:
            gather_copy(which, own, whole, d).start()
        whole[me] = own[...]

    def gather_forward(which, own, whole):
        for d in range(1, chips):
            gather_copy(which, own, whole, d).wait_recv()
            forward_copy(which, whole, d).start()

    def gather_end(which, own, whole):
        gather_copy(which, own, whole, 0).wait_recv()
        for d in range(1, chips):
            forward_copy(which, whole, d).wait_recv()
        for d in range(chips):
            gather_copy(which, own, whole, d).wait_send()
        for d in range(1, chips):
            forward_copy(which, whole, d).wait_send()

    def right_copy(scan, k):
        own, to_right, to_left, from_left, from_right, sems = scan
        return pltpu.make_async_remote_copy(
            src_ref=to_right.at[k], dst_ref=from_left.at[k],
            send_sem=sems.at[0, k], recv_sem=sems.at[1, k],
            device_id=(lax.rem(z + 1, rows_n), me), device_id_type=MESH,
        )

    def left_copy(scan, k):
        own, to_right, to_left, from_left, from_right, sems = scan
        return pltpu.make_async_remote_copy(
            src_ref=to_left.at[k], dst_ref=from_right.at[k],
            send_sem=sems.at[2, k], recv_sem=sems.at[3, k],
            device_id=(lax.rem(z + last, rows_n), me), device_id_type=MESH,
        )

    def scan_step(scan, it):
        own, to_right, to_left, from_left, from_right, sems = scan
        kr = it - LAG * z
        kl = it - LAG * (last - z)

        @pl.when((kr >= 0) & (kr < chunks) & (z < last))
        def _():
            @pl.when(z == 0)
            def _():
                to_right[kr] = own[kr].astype(BF16)

            @pl.when(z > 0)
            def _():
                right_copy(scan, kr).wait_recv()
                to_right[kr] = (own[kr].astype(F32) + from_left[kr].astype(F32)).astype(BF16)

            right_copy(scan, kr).start()

        @pl.when((kl >= 0) & (kl < chunks) & (z > 0))
        def _():
            @pl.when(z == last)
            def _():
                to_left[kl] = own[kl].astype(BF16)

            @pl.when(z < last)
            def _():
                left_copy(scan, kl).wait_recv()
                to_left[kl] = (own[kl].astype(F32) + from_right[kl].astype(F32)).astype(BF16)

            left_copy(scan, kl).start()

    def scan_total(scan, k):
        own, to_right, to_left, from_left, from_right, sems = scan

        @pl.when(z == last)
        def _():
            right_copy(scan, k).wait_recv()

        @pl.when(z == 0)
        def _():
            left_copy(scan, k).wait_recv()

        @pl.when(z > 0)
        def _():
            own[k] = (own[k].astype(F32) + from_left[k].astype(F32)).astype(own.dtype)

        @pl.when(z < last)
        def _():
            own[k] = (own[k].astype(F32) + from_right[k].astype(F32)).astype(own.dtype)

    def scan_sent(scan):
        @pl.loop(0, chunks)
        def _(k):
            @pl.when(z < last)
            def _():
                right_copy(scan, k).wait_send()

            @pl.when(z > 0)
            def _():
                left_copy(scan, k).wait_send()

    def across_copy(buffers, h, q):
        send_a, recv_a, send_b, recv_b, sems = buffers
        return pltpu.make_async_remote_copy(
            src_ref=send_a.at[h, q], dst_ref=recv_a.at[h, q],
            send_sem=sems.at[h, 0, q], recv_sem=sems.at[h, 1, q],
            device_id=(z, other), device_id_type=MESH,
        )

    def between_copy(buffers, h, d):
        send_a, recv_a, send_b, recv_b, sems = buffers
        return pltpu.make_async_remote_copy(
            src_ref=send_b.at[h, d], dst_ref=recv_b.at[h, d],
            send_sem=sems.at[h, 2, d], recv_sem=sems.at[h, 3, d],
            device_id=(z, chip_at(d) * 2 + core), device_id_type=MESH,
        )

    def scatter_start(mine, buffers):
        send_a, recv_a, send_b, recv_b, sems = buffers
        for h in range(send_a.shape[0]):
            for d in list(range(1, chips)) + [0]:
                q = chip_at(d)
                send_a[h, q] = mine(h, q * 2 + (1 - core)).astype(BF16)
                across_copy(buffers, h, q).start()
        for h in range(send_a.shape[0]):
            for d in range(1, chips):
                q = chip_at(d)
                across_copy(buffers, h, q).wait_recv()
                send_b[h, d] = (mine(h, q * 2 + core) + recv_a[h, q].astype(F32)).astype(BF16)
                between_copy(buffers, h, d).start()

    def scatter_end(mine, buffers, h):
        send_a, recv_a, send_b, recv_b, sems = buffers
        across_copy(buffers, h, chip).wait_recv()
        total = mine(h, me) + recv_a[h, chip].astype(F32)
        for d in range(1, chips):
            between_copy(buffers, h, d).wait_recv()
            total = total + recv_b[h, d].astype(F32)
        return total

    def scatter_sent(buffers):
        for h in range(buffers[0].shape[0]):
            for d in range(chips):
                across_copy(buffers, h, chip_at(d)).wait_send()
            for d in range(1, chips):
                between_copy(buffers, h, d).wait_send()

    gather_start(0, dir_own, dir_all)

    point_block = rows_here // chunks

    for b in range(chunks):
        here = slice(b * point_block, (b + 1) * point_block)
        points = x_ref[:, here] * POINT_SCALE
        high = points.astype(BF16)
        xhl_t[:FEAT, here] = high
        xhl_t[FEAT:, here] = (points - high.astype(F32)).astype(BF16)

    def augmented(pair, norm_at, one_at):
        high = pair[:FEAT]
        low = pair[FEAT:]
        exact = high + low
        half = -0.5 * jnp.sum(exact * exact, axis=0, keepdims=True)
        sub = lax.broadcasted_iota(jnp.int32, high.shape, 0)
        extra = jnp.where((sub >= one_at) & (sub < one_at + 3), 1.0, 0.0)
        for at, term in enumerate(three(half)):
            extra = jnp.where(sub == norm_at + at, term, extra)
        return high, low, extra

    def augment(b):
        here = pl.ds(pl.multiple_of(b * point_block, point_block), point_block)
        high, low, extra = augmented(xhl_t[:, here].astype(F32), 0, 3)
        xaug[here, :] = jnp.concatenate([high, low, high, extra], axis=0).T.astype(BF16)

    pick_block = math.gcd(rows_here, 1024)

    @pl.loop(0, chunks)
    def _(it):
        wanted = idx_ref[it] - z * rows_here
        total = jnp.zeros((2 * FEAT, CHUNK), F32)
        for b in range(rows_here // pick_block):
            ids = lax.broadcasted_iota(jnp.int32, (pick_block, CHUNK), 0) + b * pick_block
            hot = jnp.where(ids == wanted, 1.0, 0.0).astype(BF16)
            total = total + dot(xhl_t[:, b * pick_block : (b + 1) * pick_block], hot)
        pick[0][it] = total.astype(BF16)
        scan_step(pick, it)
        augment(it)

    gather_forward(0, dir_own, dir_all)
    gather_end(0, dir_own, dir_all)

    fit_acc[...] = jnp.zeros_like(fit_acc)
    k_block = math.gcd(rows_here, 512)

    @pl.loop(0, chunks + LAG * last)
    def _(it):
        scan_step(pick, it + chunks)

        @pl.when(it < chunks)
        def _():
            p_copy(it).wait()
            directions = dir_all[...].reshape(cent_n * part, OUTS)
            coef[0][it] = dot(p_buf[it], directions)

        scan_step(coef, it)

        @pl.when(it < chunks)
        def _():
            scan_total(pick, it)
            high, low, extra = augmented(pick[0][it].astype(F32), 3, 0)
            caug_t[...] = jnp.concatenate([high, high, low, extra], axis=0).astype(BF16)

            for b in range(rows_here // k_block):
                here = slice(b * k_block, (b + 1) * k_block)
                k_buf[it, here, :] = jnp.exp(dot(xaug[here, :], caug_t[...])).astype(BF16)

        @pl.when(it >= LAG * last)
        def _():
            k = it - LAG * last
            scan_total(coef, k)
            coef_low[...] = coef[0][k].astype(BF16)

            for b in range(cent_n):
                here = slice(b * fit_part, (b + 1) * fit_part)
                fit_acc[b] += dot(k_buf[k, here, :], coef_low[...])

    fit_pieces = fit_own.shape[0]
    fit_piece = fit_part // fit_pieces

    def fit_mine(h, block):
        return fit_acc[block, h * fit_piece : (h + 1) * fit_piece, :]

    scatter_start(fit_mine, fit_rs)
    for h in range(fit_pieces):
        fit_own[h] = scatter_end(fit_mine, fit_rs, h).T.astype(BF16)
        gather_start(1 + h, fit_own.at[h], fit_all.at[h])
    img_acc[...] = jnp.zeros_like(img_acc)
    for h in range(fit_pieces):
        gather_forward(1 + h, fit_own.at[h], fit_all.at[h])
    for h in range(fit_pieces):
        gather_end(1 + h, fit_own.at[h], fit_all.at[h])
    scatter_sent(fit_rs)

    scale = float(rows_here * rows_n) ** -0.5

    @pl.loop(0, chunks + LAG * last)
    def _(it):
        @pl.when(it < chunks)
        def _():
            total = jnp.zeros((OUTS, CHUNK), F32)
            for b in range(cent_n):
                for h in range(fit_pieces):
                    start = b * fit_part + h * fit_piece
                    total = total + dot(fit_all[h, b], k_buf[it, start : start + fit_piece, :])
            grad[0][it] = total

        scan_step(grad, it)

        @pl.when(it >= LAG * last)
        def _():
            k = it - LAG * last
            scan_total(grad, k)
            low = (grad[0][k] * scale).astype(BF16)
            for b in range(cent_n):
                img_acc[b] += dot(low, p_buf[k, :, b * part : (b + 1) * part])

    img_pieces = img_rs[0].shape[0]
    img_piece = part // img_pieces

    def img_mine(h, block):
        return img_acc[block, :, h * img_piece : (h + 1) * img_piece]

    scatter_start(img_mine, img_rs)
    image = jnp.concatenate(
        [scatter_end(img_mine, img_rs, h).T for h in range(img_pieces)], axis=0
    )
    image = image + ridge_weight * dir_ref[...]
    image_ref[...] = image

    def rows_sum(value):
        return jnp.sum(value, axis=0, keepdims=True)

    residual = res_ref[...]
    sc_own[...] = jnp.concatenate(
        [
            rows_sum(residual * residual),
            rows_sum(dir_ref[...] * image),
            rows_sum(residual * image),
            rows_sum(image * image),
            jnp.zeros((4, OUTS), F32),
        ],
        axis=0,
    )

    def cent_copy(d):
        return pltpu.make_async_remote_copy(
            src_ref=sc_own, dst_ref=sc_cent.at[d],
            send_sem=sc_sems.at[0, d], recv_sem=sc_sems.at[1, d],
            device_id=(z, lax.rem(me + d, cent_n)), device_id_type=MESH,
        )

    def rows_copy(d):
        return pltpu.make_async_remote_copy(
            src_ref=sc_mid, dst_ref=sc_rows.at[d],
            send_sem=sc_sems.at[2, d], recv_sem=sc_sems.at[3, d],
            device_id=(lax.rem(z + d, rows_n), me), device_id_type=MESH,
        )

    for d in range(1, cent_n):
        cent_copy(d).start()
    total = sc_own[...]
    for d in range(1, cent_n):
        cent_copy(d).wait_recv()
        total = total + sc_cent[d]
    sc_mid[...] = total
    for d in range(1, rows_n):
        rows_copy(d).start()
    for d in range(1, rows_n):
        rows_copy(d).wait_recv()
        total = total + sc_rows[d]
    sums_ref[...] = total

    for d in range(1, cent_n):
        cent_copy(d).wait_send()
    for d in range(1, rows_n):
        rows_copy(d).wait_send()
    scan_sent(pick)
    scan_sent(coef)
    scan_sent(grad)
    scatter_sent(img_rs)


def update_kernel(sums_ref, image_ref, coef_ref, res_ref, dir_ref, coef_out, res_out, dir_out):
    totals = jnp.sum(sums_ref[...], axis=1, keepdims=True)
    norm_old, curvature, cross, square = (totals[at : at + 1] for at in range(4))
    step_size = norm_old / curvature
    norm_new = norm_old - 2.0 * step_size * cross + step_size * step_size * square
    ratio = norm_new / norm_old
    direction = dir_ref[...]
    coef_out[...] = coef_ref[...] + step_size * direction
    residual_next = res_ref[...] - step_size * image_ref[...]
    res_out[...] = residual_next
    dir_out[...] = residual_next + ratio * direction


def on_device(rows_n, cent_n, train_rows, centre_index, precond, coefficients, residual, direction):
    rows_here = train_rows.shape[0]
    centres_here = centre_index.shape[0]
    part = direction.shape[0]
    chunks = centres_here // CHUNK
    chips = cent_n // 2
    fit_part = rows_here // cent_n
    fit_pieces = 2 if fit_part % 256 == 0 else 1
    img_pieces = 2 if part % 256 == 0 else 1
    vmem = pl.BlockSpec(memory_space=pltpu.VMEM)

    def scan(shape, own_dtype):
        piece = (chunks,) + shape
        return (
            pltpu.VMEM(piece, own_dtype),
            pltpu.VMEM(piece, BF16), pltpu.VMEM(piece, BF16),
            pltpu.VMEM(piece, BF16), pltpu.VMEM(piece, BF16),
            pltpu.SemaphoreType.DMA((4, chunks)),
        )

    def scatter(pieces, shape):
        piece = (pieces, chips) + shape
        return (
            pltpu.VMEM(piece, BF16), pltpu.VMEM(piece, BF16),
            pltpu.VMEM(piece, BF16), pltpu.VMEM(piece, BF16),
            pltpu.SemaphoreType.DMA((pieces, 4, chips)),
        )

    image, sums = pl.pallas_call(
        functools.partial(step_kernel, rows_n, cent_n),
        out_shape=(
            jax.ShapeDtypeStruct((part, OUTS), F32),
            jax.ShapeDtypeStruct((8, OUTS), F32),
        ),
        in_specs=[vmem, vmem, pl.BlockSpec(memory_space=pl.ANY), vmem, vmem],
        out_specs=(vmem, vmem),
        scratch_shapes=[
            pltpu.VMEM((chunks, CHUNK, precond.shape[1]), BF16),
            pltpu.SemaphoreType.DMA((chunks,)),
            pltpu.VMEM((chunks, rows_here, CHUNK), BF16),
            pltpu.VMEM((rows_here, 4 * FEAT), BF16),
            pltpu.VMEM((2 * FEAT, rows_here), BF16),
            pltpu.VMEM((4 * FEAT, CHUNK), BF16),
            scan((2 * FEAT, CHUNK), BF16),
            scan((CHUNK, OUTS), F32),
            scan((OUTS, CHUNK), F32),
            pltpu.VMEM((CHUNK, OUTS), BF16),
            pltpu.VMEM((part, OUTS), BF16),
            pltpu.VMEM((cent_n, part, OUTS), BF16),
            pltpu.VMEM((fit_pieces, OUTS, fit_part // fit_pieces), BF16),
            pltpu.VMEM((fit_pieces, cent_n, OUTS, fit_part // fit_pieces), BF16),
            pltpu.SemaphoreType.DMA((1 + fit_pieces, 4, chips)),
            pltpu.VMEM((cent_n, fit_part, OUTS), F32),
            scatter(fit_pieces, (fit_part // fit_pieces, OUTS)),
            pltpu.VMEM((cent_n, OUTS, part), F32),
            scatter(img_pieces, (OUTS, part // img_pieces)),
            pltpu.VMEM((8, OUTS), F32),
            pltpu.VMEM((cent_n, 8, OUTS), F32),
            pltpu.VMEM((8, OUTS), F32),
            pltpu.VMEM((rows_n, 8, OUTS), F32),
            pltpu.SemaphoreType.DMA((4, max(cent_n, rows_n))),
        ],
        compiler_params=pltpu.CompilerParams(
            collective_id=0, has_side_effects=True, vmem_limit_bytes=67000000
        ),
        name="falkon_step",
    )(centre_index.reshape(chunks, 1, CHUNK), train_rows.T, precond, residual, direction)

    piece = jax.ShapeDtypeStruct((part, OUTS), F32)
    return pl.pallas_call(
        update_kernel,
        out_shape=(piece, piece, piece),
        in_specs=[vmem] * 5,
        out_specs=(vmem, vmem, vmem),
        name="falkon_update",
    )(sums, image, coefficients, residual, direction)


def solution(mesh):
    both = P(("rows", "cent"), None)
    return jax.shard_map(
        functools.partial(on_device, mesh.shape["rows"], mesh.shape["cent"]),
        mesh=mesh,
        in_specs=(P("rows", None), P("cent"), P("cent", "rows"), both, both, both),
        out_specs=(both, both, both),
        check_vma=False,
    )
```

```python
import functools
import math

import jax
import jax.numpy as jnp
from jax import lax
from jax.experimental import pallas as pl
from jax.experimental.pallas import tpu as pltpu
from jax.sharding import PartitionSpec as P

FEAT = 64
OUTS = 128
CHUNK = 256
LAG = 4
F32 = jnp.float32
BF16 = jnp.bfloat16
MESH = pl.DeviceIdType.MESH
POINT_SCALE = math.sqrt(4.0 / FEAT)

ridge_weight = 0.1


def dot(a, b):
    return jnp.dot(a, b, preferred_element_type=F32)


def three(value):
    high = value.astype(BF16)
    rest = value - high.astype(F32)
    middle = rest.astype(BF16)
    low = (rest - middle.astype(F32)).astype(BF16)
    return high.astype(F32), middle.astype(F32), low.astype(F32)


def step_kernel(
    rows_n, cent_n,
    idx_ref, x_ref, p_hbm, res_ref, dir_ref,
    image_ref, sums_ref,
    p_buf, p_sem, k_buf, xaug, xhl_t, caug_t,
    pick, coef, grad, coef_low,
    dir_own, dir_all, fit_own, fit_all, gather_sems,
    fit_acc, fit_rs, img_acc, img_rs,
    sc_own, sc_cent, sc_mid, sc_rows, sc_sems,
):
    z = lax.axis_index("rows")
    me = lax.axis_index("cent")
    core = lax.rem(me, 2)
    chip = lax.div(me, 2)
    other = chip * 2 + (1 - core)
    chips = cent_n // 2
    chunks = p_buf.shape[0]
    rows_here = x_ref.shape[1]
    part = dir_own.shape[0]
    fit_part = fit_acc.shape[1]
    last = rows_n - 1

    def chip_at(distance):
        return lax.rem(chip + distance, chips)

    def p_copy(k):
        return pltpu.make_async_copy(
            p_hbm.at[pl.ds(pl.multiple_of(k * CHUNK, CHUNK), CHUNK)], p_buf.at[k], p_sem.at[k]
        )

    @pl.loop(0, chunks)
    def _(k):
        p_copy(k).start()

    barrier = pltpu.get_barrier_semaphore()
    for d in range(1, cent_n):
        pl.semaphore_signal(
            barrier, inc=1, device_id=(z, lax.rem(me + d, cent_n)), device_id_type=MESH
        )
    for d in range(1, rows_n):
        pl.semaphore_signal(
            barrier, inc=1, device_id=(lax.rem(z + d, rows_n), me), device_id_type=MESH
        )
    dir_own[...] = dir_ref[...].astype(BF16)
    pl.semaphore_wait(barrier, cent_n - 1 + rows_n - 1)

    def gather_copy(which, own, whole, d):
        target = other if d == 0 else chip_at(d) * 2 + core
        return pltpu.make_async_remote_copy(
            src_ref=own, dst_ref=whole.at[me],
            send_sem=gather_sems.at[which, 0, d], recv_sem=gather_sems.at[which, 1, d],
            device_id=(z, target), device_id_type=MESH,
        )

    def forward_copy(which, whole, d):
        source = chip_at(chips - d) * 2 + core
        return pltpu.make_async_remote_copy(
            src_ref=whole.at[source], dst_ref=whole.at[source],
            send_sem=gather_sems.at[which, 2, d], recv_sem=gather_sems.at[which, 3, d],
            device_id=(z, other), device_id_type=MESH,
        )

    def gather_start(which, own, whole):
        for d in list(range(1, chips)) + [0]:
            gather_copy(which, own, whole, d).start()
        whole[me] = own[...]

    def gather_forward(which, own, whole):
        for d in range(1, chips):
            gather_copy(which, own, whole, d).wait_recv()
            forward_copy(which, whole, d).start()

    def gather_end(which, own, whole):
        gather_copy(which, own, whole, 0).wait_recv()
        for d in range(1, chips):
            forward_copy(which, whole, d).wait_recv()
        for d in range(chips):
            gather_copy(which, own, whole, d).wait_send()
        for d in range(1, chips):
            forward_copy(which, whole, d).wait_send()

    def right_copy(scan, k):
        own, to_right, to_left, from_left, from_right, sems = scan
        return pltpu.make_async_remote_copy(
            src_ref=to_right.at[k], dst_ref=from_left.at[k],
            send_sem=sems.at[0, k], recv_sem=sems.at[1, k],
            device_id=(lax.rem(z + 1, rows_n), me), device_id_type=MESH,
        )

    def left_copy(scan, k):
        own, to_right, to_left, from_left, from_right, sems = scan
        return pltpu.make_async_remote_copy(
            src_ref=to_left.at[k], dst_ref=from_right.at[k],
            send_sem=sems.at[2, k], recv_sem=sems.at[3, k],
            device_id=(lax.rem(z + last, rows_n), me), device_id_type=MESH,
        )

    def scan_step(scan, it):
        own, to_right, to_left, from_left, from_right, sems = scan
        kr = it - LAG * z
        kl = it - LAG * (last - z)

        @pl.when((kr >= 0) & (kr < chunks) & (z < last))
        def _():
            @pl.when(z == 0)
            def _():
                to_right[kr] = own[kr].astype(BF16)

            @pl.when(z > 0)
            def _():
                right_copy(scan, kr).wait_recv()
                to_right[kr] = (own[kr].astype(F32) + from_left[kr].astype(F32)).astype(BF16)

            right_copy(scan, kr).start()

        @pl.when((kl >= 0) & (kl < chunks) & (z > 0))
        def _():
            @pl.when(z == last)
            def _():
                to_left[kl] = own[kl].astype(BF16)

            @pl.when(z < last)
            def _():
                left_copy(scan, kl).wait_recv()
                to_left[kl] = (own[kl].astype(F32) + from_right[kl].astype(F32)).astype(BF16)

            left_copy(scan, kl).start()

    def scan_total(scan, k):
        own, to_right, to_left, from_left, from_right, sems = scan

        @pl.when(z == last)
        def _():
            right_copy(scan, k).wait_recv()

        @pl.when(z == 0)
        def _():
            left_copy(scan, k).wait_recv()

        @pl.when(z > 0)
        def _():
            own[k] = (own[k].astype(F32) + from_left[k].astype(F32)).astype(own.dtype)

        @pl.when(z < last)
        def _():
            own[k] = (own[k].astype(F32) + from_right[k].astype(F32)).astype(own.dtype)

    def scan_sent(scan):
        @pl.loop(0, chunks)
        def _(k):
            @pl.when(z < last)
            def _():
                right_copy(scan, k).wait_send()

            @pl.when(z > 0)
            def _():
                left_copy(scan, k).wait_send()

    def across_copy(buffers, h, q):
        send_a, recv_a, send_b, recv_b, sems = buffers
        return pltpu.make_async_remote_copy(
            src_ref=send_a.at[h, q], dst_ref=recv_a.at[h, q],
            send_sem=sems.at[h, 0, q], recv_sem=sems.at[h, 1, q],
            device_id=(z, other), device_id_type=MESH,
        )

    def between_copy(buffers, h, d):
        send_a, recv_a, send_b, recv_b, sems = buffers
        return pltpu.make_async_remote_copy(
            src_ref=send_b.at[h, d], dst_ref=recv_b.at[h, d],
            send_sem=sems.at[h, 2, d], recv_sem=sems.at[h, 3, d],
            device_id=(z, chip_at(d) * 2 + core), device_id_type=MESH,
        )

    def scatter_start(mine, buffers):
        send_a, recv_a, send_b, recv_b, sems = buffers
        for h in range(send_a.shape[0]):
            for d in list(range(1, chips)) + [0]:
                q = chip_at(d)
                send_a[h, q] = mine(h, q * 2 + (1 - core)).astype(BF16)
                across_copy(buffers, h, q).start()
        for h in range(send_a.shape[0]):
            for d in range(1, chips):
                q = chip_at(d)
                across_copy(buffers, h, q).wait_recv()
                send_b[h, d] = (mine(h, q * 2 + core) + recv_a[h, q].astype(F32)).astype(BF16)
                between_copy(buffers, h, d).start()

    def scatter_end(mine, buffers, h):
        send_a, recv_a, send_b, recv_b, sems = buffers
        across_copy(buffers, h, chip).wait_recv()
        total = mine(h, me) + recv_a[h, chip].astype(F32)
        for d in range(1, chips):
            between_copy(buffers, h, d).wait_recv()
            total = total + recv_b[h, d].astype(F32)
        return total

    def scatter_sent(buffers):
        for h in range(buffers[0].shape[0]):
            for d in range(chips):
                across_copy(buffers, h, chip_at(d)).wait_send()
            for d in range(1, chips):
                between_copy(buffers, h, d).wait_send()

    gather_start(0, dir_own, dir_all)

    point_block = rows_here // chunks

    for b in range(chunks):
        here = slice(b * point_block, (b + 1) * point_block)
        points = x_ref[:, here] * POINT_SCALE
        high = points.astype(BF16)
        xhl_t[:FEAT, here] = high
        xhl_t[FEAT:, here] = (points - high.astype(F32)).astype(BF16)

    def augmented(pair, norm_at, one_at):
        high = pair[:FEAT]
        low = pair[FEAT:]
        exact = high + low
        half = -0.5 * jnp.sum(exact * exact, axis=0, keepdims=True)
        sub = lax.broadcasted_iota(jnp.int32, high.shape, 0)
        extra = jnp.where((sub >= one_at) & (sub < one_at + 3), 1.0, 0.0)
        for at, term in enumerate(three(half)):
            extra = jnp.where(sub == norm_at + at, term, extra)
        return high, low, extra

    def augment(b):
        here = pl.ds(pl.multiple_of(b * point_block, point_block), point_block)
        high, low, extra = augmented(xhl_t[:, here].astype(F32), 0, 3)
        xaug[here, :] = jnp.concatenate([high, low, high, extra], axis=0).T.astype(BF16)

    pick_block = math.gcd(rows_here, 1024)

    @pl.loop(0, chunks)
    def _(it):
        wanted = idx_ref[it] - z * rows_here
        total = jnp.zeros((2 * FEAT, CHUNK), F32)
        for b in range(rows_here // pick_block):
            ids = lax.broadcasted_iota(jnp.int32, (pick_block, CHUNK), 0) + b * pick_block
            hot = jnp.where(ids == wanted, 1.0, 0.0).astype(BF16)
            total = total + dot(xhl_t[:, b * pick_block : (b + 1) * pick_block], hot)
        pick[0][it] = total.astype(BF16)
        scan_step(pick, it)
        augment(it)

    gather_forward(0, dir_own, dir_all)
    gather_end(0, dir_own, dir_all)

    fit_acc[...] = jnp.zeros_like(fit_acc)
    k_block = math.gcd(rows_here, 512)

    @pl.loop(0, chunks + LAG * last)
    def _(it):
        scan_step(pick, it + chunks)

        @pl.when(it < chunks)
        def _():
            p_copy(it).wait()
            directions = dir_all[...].reshape(cent_n * part, OUTS)
            coef[0][it] = dot(p_buf[it], directions)

        scan_step(coef, it)

        @pl.when(it < chunks)
        def _():
            scan_total(pick, it)
            high, low, extra = augmented(pick[0][it].astype(F32), 3, 0)
            caug_t[...] = jnp.concatenate([high, high, low, extra], axis=0).astype(BF16)

            for b in range(rows_here // k_block):
                here = slice(b * k_block, (b + 1) * k_block)
                k_buf[it, here, :] = jnp.exp(dot(xaug[here, :], caug_t[...])).astype(BF16)

        @pl.when(it >= LAG * last)
        def _():
            k = it - LAG * last
            scan_total(coef, k)
            coef_low[...] = coef[0][k].astype(BF16)

            for b in range(cent_n):
                here = slice(b * fit_part, (b + 1) * fit_part)
                fit_acc[b] += dot(k_buf[k, here, :], coef_low[...])

    fit_pieces = fit_own.shape[0]
    fit_piece = fit_part // fit_pieces

    def fit_mine(h, block):
        return fit_acc[block, h * fit_piece : (h + 1) * fit_piece, :]

    scatter_start(fit_mine, fit_rs)
    for h in range(fit_pieces):
        fit_own[h] = scatter_end(fit_mine, fit_rs, h).T.astype(BF16)
        gather_start(1 + h, fit_own.at[h], fit_all.at[h])
    img_acc[...] = jnp.zeros_like(img_acc)
    for h in range(fit_pieces):
        gather_forward(1 + h, fit_own.at[h], fit_all.at[h])
    for h in range(fit_pieces):
        gather_end(1 + h, fit_own.at[h], fit_all.at[h])
    scatter_sent(fit_rs)

    scale = float(rows_here * rows_n) ** -0.5

    @pl.loop(0, chunks + LAG * last)
    def _(it):
        @pl.when(it < chunks)
        def _():
            total = jnp.zeros((OUTS, CHUNK), F32)
            for b in range(cent_n):
                for h in range(fit_pieces):
                    start = b * fit_part + h * fit_piece
                    total = total + dot(fit_all[h, b], k_buf[it, start : start + fit_piece, :])
            grad[0][it] = total

        scan_step(grad, it)

        @pl.when(it >= LAG * last)
        def _():
            k = it - LAG * last
            scan_total(grad, k)
            low = (grad[0][k] * scale).astype(BF16)
            for b in range(cent_n):
                img_acc[b] += dot(low, p_buf[k, :, b * part : (b + 1) * part])

    img_pieces = img_rs[0].shape[0]
    img_piece = part // img_pieces

    def img_mine(h, block):
        return img_acc[block, :, h * img_piece : (h + 1) * img_piece]

    scatter_start(img_mine, img_rs)
    image = jnp.concatenate(
        [scatter_end(img_mine, img_rs, h).T for h in range(img_pieces)], axis=0
    )
    image = image + ridge_weight * dir_ref[...]
    image_ref[...] = image

    def rows_sum(value):
        return jnp.sum(value, axis=0, keepdims=True)

    residual = res_ref[...]
    sc_own[...] = jnp.concatenate(
        [
            rows_sum(residual * residual),
            rows_sum(dir_ref[...] * image),
            rows_sum(residual * image),
            rows_sum(image * image),
            jnp.zeros((4, OUTS), F32),
        ],
        axis=0,
    )

    def cent_copy(d):
        return pltpu.make_async_remote_copy(
            src_ref=sc_own, dst_ref=sc_cent.at[d],
            send_sem=sc_sems.at[0, d], recv_sem=sc_sems.at[1, d],
            device_id=(z, lax.rem(me + d, cent_n)), device_id_type=MESH,
        )

    def rows_copy(d):
        return pltpu.make_async_remote_copy(
            src_ref=sc_mid, dst_ref=sc_rows.at[d],
            send_sem=sc_sems.at[2, d], recv_sem=sc_sems.at[3, d],
            device_id=(lax.rem(z + d, rows_n), me), device_id_type=MESH,
        )

    for d in range(1, cent_n):
        cent_copy(d).start()
    total = sc_own[...]
    for d in range(1, cent_n):
        cent_copy(d).wait_recv()
        total = total + sc_cent[d]
    sc_mid[...] = total
    for d in range(1, rows_n):
        rows_copy(d).start()
    for d in range(1, rows_n):
        rows_copy(d).wait_recv()
        total = total + sc_rows[d]
    sums_ref[...] = total

    for d in range(1, cent_n):
        cent_copy(d).wait_send()
    for d in range(1, rows_n):
        rows_copy(d).wait_send()
    scan_sent(pick)
    scan_sent(coef)
    scan_sent(grad)
    scatter_sent(img_rs)


def update_kernel(sums_ref, image_ref, coef_ref, res_ref, dir_ref, coef_out, res_out, dir_out):
    totals = jnp.sum(sums_ref[...], axis=1, keepdims=True)
    norm_old, curvature, cross, square = (totals[at : at + 1] for at in range(4))
    step_size = norm_old / curvature
    norm_new = norm_old - 2.0 * step_size * cross + step_size * step_size * square
    ratio = norm_new / norm_old
    direction = dir_ref[...]
    coef_out[...] = coef_ref[...] + step_size * direction
    residual_next = res_ref[...] - step_size * image_ref[...]
    res_out[...] = residual_next
    dir_out[...] = residual_next + ratio * direction


def on_device(rows_n, cent_n, train_rows, centre_index, precond, coefficients, residual, direction):
    rows_here = train_rows.shape[0]
    centres_here = centre_index.shape[0]
    part = direction.shape[0]
    chunks = centres_here // CHUNK
    chips = cent_n // 2
    fit_part = rows_here // cent_n
    fit_pieces = 2 if fit_part % 256 == 0 else 1
    img_pieces = 2 if part % 256 == 0 else 1
    vmem = pl.BlockSpec(memory_space=pltpu.VMEM)

    def scan(shape, own_dtype):
        piece = (chunks,) + shape
        return (
            pltpu.VMEM(piece, own_dtype),
            pltpu.VMEM(piece, BF16), pltpu.VMEM(piece, BF16),
            pltpu.VMEM(piece, BF16), pltpu.VMEM(piece, BF16),
            pltpu.SemaphoreType.DMA((4, chunks)),
        )

    def scatter(pieces, shape):
        piece = (pieces, chips) + shape
        return (
            pltpu.VMEM(piece, BF16), pltpu.VMEM(piece, BF16),
            pltpu.VMEM(piece, BF16), pltpu.VMEM(piece, BF16),
            pltpu.SemaphoreType.DMA((pieces, 4, chips)),
        )

    image, sums = pl.pallas_call(
        functools.partial(step_kernel, rows_n, cent_n),
        out_shape=(
            jax.ShapeDtypeStruct((part, OUTS), F32),
            jax.ShapeDtypeStruct((8, OUTS), F32),
        ),
        in_specs=[vmem, vmem, pl.BlockSpec(memory_space=pl.ANY), vmem, vmem],
        out_specs=(vmem, vmem),
        scratch_shapes=[
            pltpu.VMEM((chunks, CHUNK, precond.shape[1]), BF16),
            pltpu.SemaphoreType.DMA((chunks,)),
            pltpu.VMEM((chunks, rows_here, CHUNK), BF16),
            pltpu.VMEM((rows_here, 4 * FEAT), BF16),
            pltpu.VMEM((2 * FEAT, rows_here), BF16),
            pltpu.VMEM((4 * FEAT, CHUNK), BF16),
            scan((2 * FEAT, CHUNK), BF16),
            scan((CHUNK, OUTS), F32),
            scan((OUTS, CHUNK), F32),
            pltpu.VMEM((CHUNK, OUTS), BF16),
            pltpu.VMEM((part, OUTS), BF16),
            pltpu.VMEM((cent_n, part, OUTS), BF16),
            pltpu.VMEM((fit_pieces, OUTS, fit_part // fit_pieces), BF16),
            pltpu.VMEM((fit_pieces, cent_n, OUTS, fit_part // fit_pieces), BF16),
            pltpu.SemaphoreType.DMA((1 + fit_pieces, 4, chips)),
            pltpu.VMEM((cent_n, fit_part, OUTS), F32),
            scatter(fit_pieces, (fit_part // fit_pieces, OUTS)),
            pltpu.VMEM((cent_n, OUTS, part), F32),
            scatter(img_pieces, (OUTS, part // img_pieces)),
            pltpu.VMEM((8, OUTS), F32),
            pltpu.VMEM((cent_n, 8, OUTS), F32),
            pltpu.VMEM((8, OUTS), F32),
            pltpu.VMEM((rows_n, 8, OUTS), F32),
            pltpu.SemaphoreType.DMA((4, max(cent_n, rows_n))),
        ],
        compiler_params=pltpu.CompilerParams(
            collective_id=0, has_side_effects=True, vmem_limit_bytes=67000000
        ),
        name="falkon_step",
    )(centre_index.reshape(chunks, 1, CHUNK), train_rows.T, precond, residual, direction)

    piece = jax.ShapeDtypeStruct((part, OUTS), F32)
    return pl.pallas_call(
        update_kernel,
        out_shape=(piece, piece, piece),
        in_specs=[vmem] * 5,
        out_specs=(vmem, vmem, vmem),
        name="falkon_update",
    )(sums, image, coefficients, residual, direction)


def solution(mesh):
    both = P(("rows", "cent"), None)
    return jax.shard_map(
        functools.partial(on_device, mesh.shape["rows"], mesh.shape["cent"]),
        mesh=mesh,
        in_specs=(P("rows", None), P("cent"), P("cent", "rows"), both, both, both),
        out_specs=(both, both, both),
        check_vma=False,
    )
```
